512 devices in a mesh: loop: 64 (over z_lo, x, core), rep: 8 (over y, z_hi).
Axes of the slice: x: 4, y: 4, z: 16 (z_hi: 2, z_lo: 8; z = z_hi * 8 + z_lo), core: 2. Of those that a mesh axis runs over, the one named last changes fastest.
Arguments:
- features: bfloat16 [65536, 256], P(('loop', 'rep')), may hold values from -6 to 6
- weight: bfloat16 [256, 256], replicated, may hold values from -0.375 to 0.375
- tile_values: bfloat16 [49152, 128, 128], P(('loop', 'rep')), may hold values from -0.375 to 0.375
- tile_coords: int32 [49152, 2], P(('loop', 'rep')), may hold values from 0 to 7
- tile_counts: int32 [512, 8], P(('loop', 'rep')), may hold values from 1 to 12, as said below
Outputs:
- activated: bfloat16 [65536, 256], P(('loop', 'rep'))
The draws below stay inside these ranges and needn't reach their ends.
Inputs may be any that keep to these rules, and one draw needn't show every extreme that they name: `tile_counts`: some list uses all 12 slots at some step; loads differ strongly between lists. `tile_coords`: row block within the group's rows and column block within the slab of that step.
All inputs are finite; a program needn't handle non-finite values.
Results may differ from the reference program's by a relative error of at most 0.0049.
Values may be sent and summed in bfloat16 or wider, within the bound.
A program may use at most 64 MiB of HBM per device.

```python
import jax
import jax.numpy as jnp
from jax import lax

F = 256
R = 128
TILE = 128
SLOTS = 12
STEPS = 8
BLOCKS = 8
NODES = 65536
N_LOOP = 64
N_REP = 8


def draw_tile_counts(key, part):
    lists = N_LOOP * N_REP
    key_heavy, key_high, key_low, key_peak = jax.random.split(jax.random.fold_in(key, 7), 4)
    heavy = jax.random.randint(key_heavy, (lists, 1), 0, 4) == 0
    high = jax.random.randint(key_high, (lists, STEPS), SLOTS // 2 + 1, SLOTS + 1)
    low = jax.random.randint(key_low, (lists, STEPS), 1, max(2, SLOTS // 3 + 1))
    counts = jnp.where(heavy, high, low).reshape(-1)
    peak = jax.random.randint(key_peak, (), 0, lists * STEPS)
    counts = jnp.where(jnp.arange(lists * STEPS) == peak, SLOTS, counts)
    return counts.reshape(lists, STEPS).astype(jnp.int32)


def with_ends(drawn, key, least, largest):
    extent = drawn.shape
    spot = [jax.random.randint(jax.random.fold_in(key, axis), (), 0, extent[axis]) for axis in range(len(extent))]
    drawn = drawn.at[tuple(spot)].set(least)
    longest = extent.index(max(extent))
    spot[longest] = (spot[longest] + 1) % extent[longest]
    return drawn.at[tuple(spot)].set(largest)


def levels(own_key, shape, shards, least, largest):
    level = 1.0
    for dim, parts in shards:
        steps = jax.random.uniform(jax.random.fold_in(jax.random.fold_in(own_key, 6), dim), (parts,), jnp.float32, least / len(shards), largest / len(shards))
        level = level * jnp.repeat(jnp.exp(steps), shape[dim] // parts).reshape((-1,) + (1,) * (len(shape) - 1 - dim))
    return level


def bell_draw(rng, shape, scale, most, cuts=(), kind=jnp.bfloat16):
    factor_of = levels(rng, shape, cuts, -0.22, 0.18) if cuts else 1.0
    array = jax.random.normal(rng, shape, jnp.float32) * scale * factor_of
    return jnp.minimum(jnp.maximum(array, -most), most).astype(kind)


def setup_inputs(seed: int = 0) -> dict:
    seeds = jax.random.split(jax.random.key(seed), 6)
    return {
        "features": bell_draw(seeds[0], (NODES, F), 1.0, 6.0, ((0, 512),)),
        "weight": bell_draw(seeds[1], (F, F), F ** -0.5, 0.375),
        "tile_values": bell_draw(seeds[2], (N_LOOP * N_REP * STEPS * SLOTS, TILE, TILE), (0.3 / TILE ** 0.5), 0.375, ((0, 512),)),
        "tile_coords": with_ends(jax.random.randint(seeds[3], (N_LOOP * N_REP * STEPS * SLOTS, 2), 0, BLOCKS), jax.random.fold_in(seeds[3], 1), 0, BLOCKS - 1).astype(jnp.int32),
        "tile_counts": draw_tile_counts(jax.random.fold_in(seeds[5], 71), 0),
    }


def reference(features, weight, tile_values, tile_coords, tile_counts):
    width = features.shape[1]
    step_count = N_LOOP // N_REP
    block_count = N_REP * R // TILE
    feature_blocks = features.reshape(N_LOOP * N_REP * R // TILE, TILE, width)
    values = tile_values.reshape(N_LOOP, N_REP, step_count * SLOTS, TILE, TILE)
    coords = tile_coords.reshape(N_LOOP, N_REP, step_count, SLOTS, 2)
    counts = tile_counts.reshape(N_LOOP, N_REP, step_count)

    def group_sum(loop_index):
        def add_rank(running, rep_index):
            tile_block = values[loop_index, rep_index].astype(jnp.float32)
            coord_block = coords[loop_index, rep_index]
            count_row = counts[loop_index, rep_index]
            step_ids = jnp.arange(step_count).astype(jnp.int32)
            slab_ids = jnp.mod(loop_index - step_count * rep_index - step_ids, N_LOOP).astype(jnp.int32)
            columns = (slab_ids[:, None] * block_count + coord_block[:, :, 1]).astype(jnp.int32).reshape(-1)
            pieces = jnp.take(feature_blocks, columns, axis=0).astype(jnp.float32)
            products = jnp.einsum("ktc,kcf->ktf", tile_block, pieces, precision=lax.Precision.HIGHEST)
            live_slot = (jnp.arange(SLOTS)[None, :] < count_row[:, None]).reshape(-1)
            row_ids = coord_block[:, :, 0].reshape(-1)
            placed = ((row_ids[None, :] == jnp.arange(block_count)[:, None]) & live_slot[None, :]).astype(jnp.float32)
            running = running + jnp.einsum("bk,ktf->btf", placed, products, precision=lax.Precision.HIGHEST)
            return running, None

        start = jnp.zeros((block_count, TILE, width), jnp.float32)
        running, unused = lax.scan(add_rank, start, jnp.arange(N_REP).astype(jnp.int32))
        return running.reshape(block_count * TILE, width)

    sums = lax.map(group_sum, jnp.arange(N_LOOP).astype(jnp.int32)).reshape(-1, width)
    aggregated = sums.astype(jnp.bfloat16)
    product = jnp.dot(aggregated, weight, preferred_element_type=jnp.float32)
    return jnp.maximum(product, 0.0).astype(jnp.bfloat16)
```

```python
import functools

import jax
import jax.numpy as jnp
from jax import lax
from jax.experimental import pallas as pl
from jax.experimental.pallas import tpu as pltpu
from jax.sharding import PartitionSpec as P

MESH = pl.DeviceIdType.MESH
NX, NY, NZ, NC, NZH, NZL = 4, 4, 16, 2, 2, 8


def place():
    l = lax.axis_index("loop")
    r = lax.axis_index("rep")
    zl, x, core = l // (NX * NC), (l // NC) % NX, l % NC
    y, zh = r // NZH, r % NZH
    return x, core, y, zh * NZL + zl


def device(x, core, y, z):
    return ((z % NZL) * (NX * NC) + x * NC + core, y * NZH + z // NZL)


def greet(targets):
    barrier = pltpu.get_barrier_semaphore()
    for target in targets:
        pl.semaphore_signal(barrier, inc=1, device_id=target, device_id_type=MESH)
    pl.semaphore_wait(barrier, len(targets))


def gather_kernel(
    own, out, feat, up, down,
    up_send, up_recv, down_send, down_recv,
    y_send, y_recv, y_local, x_send, x_recv, f_send, f_recv, s_send, s_recv, o_sem,
):
    x, core, y, z = place()
    zl, zh = z % NZL, z // NZL
    xp, xm = (x + 1) % NX, (x + NX - 1) % NX
    xo = (x + 2) % NX
    zp, zm = (z + 1) % NZ, (z + NZ - 1) % NZ
    right, left = device(xp, core, y, z), device(xm, core, y, z)
    above, below = device(x, core, y, zp), device(x, core, y, zm)
    sibling = device(x, 1 - core, y, z)
    others = [(y + d) % NY for d in range(1, NY)]
    mine = x * NC + core

    def remote(src, dst, send, recv, target):
        return pltpu.make_async_remote_copy(
            src_ref=src, dst_ref=dst, send_sem=send, recv_sem=recv,
            device_id=target, device_id_type=MESH,
        )

    greet([right, left, above, below, sibling] + [device(x, core, v, z) for v in others])

    def goes(plane):
        offset = (zl + NZL - zh + NZL - plane % NZL) % NZL
        return offset // 2, offset % 2, plane // NZL

    def slab(kind):
        return (1 - kind) * mine + kind * (NX * NC)

    def hand_on(src, plane, index):
        reader, kind, half = goes(plane)
        dst = feat.at[slab(kind), half, y]

        @pl.when(reader == y)
        def _():
            pltpu.make_async_copy(src, dst, y_local.at[kind * 2 + half]).start()

        @pl.when(reader != y)
        def _():
            remote(
                src, dst, y_send.at[index], y_recv.at[kind * 2 + half, y],
                device(x, core, reader, z),
            ).start()

    def hand_on_done(src, plane, index):
        reader, kind, half = goes(plane)

        @pl.when(reader != y)
        def _():
            remote(
                src, feat.at[slab(kind), half, y], y_send.at[index],
                y_recv.at[kind * 2 + half, y], device(x, core, reader, z),
            ).wait_send()

    def x_copy(kind, half, direction):
        return remote(
            feat.at[slab(kind), half], feat.at[mine, half],
            x_send.at[direction, kind * 2 + half], x_recv.at[x, half],
            right if direction == 0 else left,
        )

    def share_copy(src, other, half):
        return remote(
            feat.at[src, half], feat.at[other * NC + core, half],
            s_send.at[other, half], s_recv.at[other, half], sibling,
        )

    def rightward(kind):
        return jnp.where(kind == 0, (x < NX - 1).astype(jnp.int32), (x == NX - 1).astype(jnp.int32)) == 1

    def leftward(kind):
        return jnp.where(kind == 0, (x == 0).astype(jnp.int32), (x > 0).astype(jnp.int32)) == 1

    def complete(src, plane):
        reader, kind, half = goes(plane)

        @pl.when(reader == y)
        def _():
            for v in others:
                remote(
                    src, feat.at[slab(kind), half, v], y_send.at[0],
                    y_recv.at[kind * 2 + half, v], sibling,
                ).wait_recv()
            pltpu.make_async_copy(
                src, feat.at[slab(kind), half, y], y_local.at[kind * 2 + half]
            ).wait()

            @pl.when(rightward(kind))
            def _():
                x_copy(kind, half, 0).start()

            @pl.when(leftward(kind))
            def _():
                x_copy(kind, half, 1).start()

            @pl.when(kind == core)
            def _():
                share_copy(slab(kind), x, half).start()

    def z_copy(src, step, upward):
        if upward:
            return remote(src, up.at[step], up_send.at[step], up_recv.at[step], above)
        return remote(src, down.at[step], down_send.at[step], down_recv.at[step], below)

    z_copy(own, 1, True).start()
    z_copy(own, 1, False).start()
    hand_on(own, z, 0)

    far = NZ // 2

    def step_body(t, carry):
        plane_up, plane_down = (z + NZ - t) % NZ, (z + t) % NZ
        z_copy(own, t, True).wait_recv()

        @pl.when(t < far)
        def _():
            z_copy(up.at[t], t + 1, True).start()
            z_copy(own, t, False).wait_recv()

            @pl.when(t < far - 1)
            def _():
                z_copy(down.at[t], t + 1, False).start()

        hand_on(up.at[t], plane_up, t)

        @pl.when(t < far)
        def _():
            hand_on(down.at[t], plane_down, far + t)

        @pl.when(t == 1)
        def _():
            complete(own, z)

        @pl.when(t > 1)
        def _():
            complete(own, (z + NZ - t + 1) % NZ)
            complete(own, (z + t - 1) % NZ)

        return carry

    lax.fori_loop(1, far + 1, step_body, 0)
    complete(own, (z + far) % NZ)

    plane_a = (zl + NZL - y * 2 - zh + NZL) % NZL
    gap = (z + NZ - plane_a) % NZ
    near = jnp.where(jnp.minimum(gap, NZ - gap) <= NZ // 4, 0, 1)

    def forward(source, half, piece, to_right):
        part = feat.at[source * NC + core, half, pl.ds(piece * 2, 2)]
        return remote(
            part, part, f_send.at[0 if to_right else 1, half, piece], f_recv.at[half, piece],
            right if to_right else left,
        )

    def arrived(source, half):
        remote(
            feat.at[mine, half], feat.at[source * NC + core, half],
            x_send.at[0, 0], x_recv.at[source, half], sibling,
        ).wait_recv()

    def out_copy(c, half):
        return pltpu.make_async_copy(feat.at[c, half], out.at[c, half], o_sem.at[c, half])

    moves = (
        (True, 0, x < NX - 1), (True, 1, x == 2), (False, 1, x > 0), (False, 0, x == 1),
    )

    for turn in range(2):
        half = jnp.where(near == turn, 0, 1)
        for to_right, source in ((True, xm), (False, xp)):
            arrived(source, half)
            for direction, piece, when in moves:
                if direction == to_right:
                    @pl.when(when)
                    def _(source=source, piece=piece, to_right=to_right):
                        forward(source, half, piece, to_right).start()
            share_copy(source * NC + core, source, half).start()
    for turn in range(2):
        half = jnp.where(near == turn, 0, 1)
        for piece in range(2):
            forward(xo, half, piece, True).wait_recv()
        share_copy(xo * NC + core, xo, half).start()
        for other in range(NX):
            out_copy(other * NC + core, half).start()
    for turn in range(2):
        half = jnp.where(near == turn, 0, 1)
        for other in (x, xm, xp, xo):
            c = other * NC + 1 - core
            remote(
                feat.at[c, half], feat.at[c, half], s_send.at[0, 0], s_recv.at[other, half], sibling
            ).wait_recv()
            out_copy(c, half).start()

    for half in range(2):
        for c in range(NX * NC):
            out_copy(c, half).wait()
        for other in range(NX):
            share_copy(other * NC + core, other, half).wait_send()
        for direction, piece, when in moves:
            @pl.when(when)
            def _(direction=direction, piece=piece, half=half):
                forward(xm if direction else xp, half, piece, direction).wait_send()
        for kind in range(2):
            @pl.when(rightward(kind))
            def _(kind=kind, half=half):
                x_copy(kind, half, 0).wait_send()

            @pl.when(leftward(kind))
            def _(kind=kind, half=half):
                x_copy(kind, half, 1).wait_send()
    hand_on_done(own, z, 0)

    def drain(t, carry):
        z_copy(own, t, True).wait_send()
        hand_on_done(up.at[t], (z + NZ - t) % NZ, t)

        @pl.when(t < far)
        def _():
            z_copy(own, t, False).wait_send()
            hand_on_done(down.at[t], (z + t) % NZ, far + t)

        return carry

    lax.fori_loop(1, far + 1, drain, 0)


def gather(features):
    rows, width = features.shape
    dma = pltpu.SemaphoreType.DMA
    kind = features.dtype
    return pl.pallas_call(
        gather_kernel,
        out_shape=jax.ShapeDtypeStruct((NX * NC, 2, NY, rows, width), kind),
        in_specs=[pl.BlockSpec(memory_space=pltpu.VMEM)],
        out_specs=pl.BlockSpec(memory_space=pl.ANY),
        scratch_shapes=[
            pltpu.VMEM((NX * NC + 1, 2, NY, rows, width), kind),
            pltpu.VMEM((NZ // 2 + 1, rows, width), kind),
            pltpu.VMEM((NZ // 2, rows, width), kind),
            dma((NZ // 2 + 1,)), dma((NZ // 2 + 1,)), dma((NZ // 2,)), dma((NZ // 2,)),
            dma((NZ,)), dma((4, NY)), dma((4,)),
            dma((2, 4)), dma((NX, 2)),
            dma((2, 2, 2)), dma((2, 2)),
            dma((NX, 2)), dma((NX, 2)),
            dma((NX * NC, 2)),
        ],
        compiler_params=pltpu.CompilerParams(collective_id=0, has_side_effects=True),
        name="gather",
    )(features)


def product_kernel(counts, coords, first, tiles, slab, out, acc, *, slots, blocks, steps):
    step = pl.program_id(0)

    @pl.when(step == 0)
    def _():
        acc[...] = jnp.zeros_like(acc)

    count = counts[step]
    for q in range(slots):
        at = (step * slots + q) * 2
        row = jnp.where(q < count, coords[at], blocks)
        b = coords[at + 1]
        spot = (b % NZH) * NY + b // NZH
        acc[row] += jnp.dot(tiles[q], slab[0, spot], preferred_element_type=jnp.float32)

    @pl.when(step == steps - 1)
    def _():
        out[...] = acc[:blocks].astype(out.dtype)


def products(tile_values, tile_coords, tile_counts, slabs):
    steps = tile_counts.shape[1]
    slots = tile_values.shape[0] // steps
    tile = tile_values.shape[1]
    width = slabs.shape[-1]
    blocks = slabs.shape[1] * slabs.shape[2]
    slabs = slabs.reshape(slabs.shape[0], blocks, tile, width)
    first = (lax.axis_index("loop") % (NX * NC)).reshape(1)
    grid = pltpu.PrefetchScalarGridSpec(
        num_scalar_prefetch=3,
        grid=(steps,),
        in_specs=[
            pl.BlockSpec((slots, tile, tile), lambda s, n, c, f: (s, 0, 0)),
            pl.BlockSpec(
                (1, blocks, tile, width), lambda s, n, c, f: ((f[0] + steps - s) % steps, 0, 0, 0)
            ),
        ],
        out_specs=pl.BlockSpec((blocks, tile, width), lambda s, n, c, f: (0, 0, 0)),
        scratch_shapes=[pltpu.VMEM((blocks + 1, tile, width), jnp.float32)],
    )
    return pl.pallas_call(
        functools.partial(product_kernel, slots=slots, blocks=blocks, steps=steps),
        grid_spec=grid,
        out_shape=jax.ShapeDtypeStruct((blocks, tile, width), slabs.dtype),
        name="products",
    )(tile_counts.reshape(-1), tile_coords.reshape(-1), first, tile_values, slabs)


def combine_kernel(part, weight, out, got, give, far, y_send, y_recv, z_send, z_recv):
    x, core, y, z = place()
    zh = z // NZL
    partner = device(x, core, y, (z + NZL) % NZ)
    others = [(y + d) % NY for d in range(1, NY)]
    greet([device(x, core, v, z) for v in others] + [partner])

    def y_copy(i, src):
        return pltpu.make_async_remote_copy(
            src_ref=part.at[others[i]], dst_ref=got.at[src], send_sem=y_send.at[i],
            recv_sem=y_recv.at[src], device_id=device(x, core, others[i], z), device_id_type=MESH,
        )

    for i in range(NY - 1):
        y_copy(i, y).start()
    for i in range(NY - 1):
        y_copy(i, others[i]).wait_recv()

    def total(half):
        held = part[y, half].astype(jnp.float32)
        for v in others:
            held += got[v, half].astype(jnp.float32)
        return held

    give[...] = total(1 - zh).astype(give.dtype)
    across = pltpu.make_async_remote_copy(
        src_ref=give, dst_ref=far, send_sem=z_send, recv_sem=z_recv,
        device_id=partner, device_id_type=MESH,
    )
    across.start()
    held = total(zh)
    across.wait()
    aggregated = (held + far[...].astype(jnp.float32)).astype(weight.dtype)
    product = jnp.dot(aggregated, weight[...], preferred_element_type=jnp.float32)
    out[...] = jnp.maximum(product, 0.0).astype(out.dtype)
    for i in range(NY - 1):
        y_copy(i, y).wait_send()


def combine(part, weight):
    blocks, rows, width = part.shape
    part = part.reshape(NY, NZH, rows, width)
    dma = pltpu.SemaphoreType.DMA
    return pl.pallas_call(
        combine_kernel,
        out_shape=jax.ShapeDtypeStruct((rows, weight.shape[1]), part.dtype),
        in_specs=[pl.BlockSpec(memory_space=pltpu.VMEM)] * 2,
        out_specs=pl.BlockSpec(memory_space=pltpu.VMEM),
        scratch_shapes=[
            pltpu.VMEM((NY, NZH, rows, width), part.dtype),
            pltpu.VMEM((rows, width), part.dtype),
            pltpu.VMEM((rows, width), part.dtype),
            dma((NY - 1,)), dma((NY,)), dma, dma,
        ],
        compiler_params=pltpu.CompilerParams(collective_id=1, has_side_effects=True),
        name="combine",
    )(part, weight)


def local(features, weight, tile_values, tile_coords, tile_counts):
    slabs = gather(features)
    part = products(tile_values, tile_coords, tile_counts, slabs)
    return combine(part, weight)


def solution(mesh):
    placed = (
        P(("loop", "rep"), None),
        P(),
        P(("loop", "rep"), None, None),
        P(("loop", "rep"), None),
        P(("loop", "rep"), None),
    )
    return jax.shard_map(
        local, mesh=mesh, in_specs=placed, out_specs=P(("loop", "rep"), None), check_vma=False
    )
```

```python
import functools

import jax
import jax.numpy as jnp
from jax import lax
from jax.experimental import pallas as pl
from jax.experimental.pallas import tpu as pltpu
from jax.sharding import PartitionSpec as P

MESH = pl.DeviceIdType.MESH
NX, NY, NZ, NC, NZH, NZL = 4, 4, 16, 2, 2, 8
STEPS = NX * NC
BLOCKS = NY * NZH
FAR = NZ // 2
PIECES = 2
LANES = 128
WIDE = NY // PIECES
Y_LAG, F_LAG = 2, 6


def place():
    l = lax.axis_index("loop")
    r = lax.axis_index("rep")
    zl, x, core = l // (NX * NC), (l // NC) % NX, l % NC
    y, zh = r // NZH, r % NZH
    return x, core, y, zh * NZL + zl


def device(x, core, y, z):
    return ((z % NZL) * (NX * NC) + x * NC + core, y * NZH + z // NZL)


def remote(src, dst, send, recv, target):
    return pltpu.make_async_remote_copy(
        src_ref=src, dst_ref=dst, send_sem=send, recv_sem=recv,
        device_id=target, device_id_type=MESH,
    )


def layer_kernel(
    counts, coords, own, weight_in, tiles_in, out,
    home, near, across, beyond, up, down, tiles, sums, give, got, hold, z_give, z_got,
    weight, draft, table,
    up_send, up_recv, down_send, down_recv, y_send, y_recv, y_local,
    x_send, x_recv, f_send, f_recv, s_send, s_recv,
    g_send, g_recv, z_send, z_recv, t_sem, w_sem, d_sem, *, slots,
):
    x, core, y, z = place()
    zl, zh = z % NZL, z // NZL
    right = device((x + 1) % NX, core, y, z)
    left = device((x + NX - 1) % NX, core, y, z)
    above = device(x, core, y, (z + 1) % NZ)
    below = device(x, core, y, (z + NZ - 1) % NZ)
    sibling = device(x, 1 - core, y, z)
    partner = device(x, core, y, (z + NZL) % NZ)
    others = [(y + d) % NY for d in range(1, NY)]
    def group(half):
        return pl.ds(half * NY, NY)

    tile_copy = pltpu.make_async_copy(tiles_in, tiles, t_sem)
    tile_copy.start()
    weight_copy = pltpu.make_async_copy(weight_in, weight, w_sem)
    weight_copy.start()

    barrier = pltpu.get_barrier_semaphore()
    friends = [right, left, above, below, sibling]
    friends += [device(x, core, v, z) for v in others]
    friends += [device(x, core, y, (z + d) % NZ) for d in (2, NZ - 2)]
    for friend in friends:
        pl.semaphore_signal(barrier, inc=1, device_id=friend, device_id_type=MESH)
    pl.semaphore_wait(barrier, len(friends))

    def z_copy(src, step, hops, upward):
        if upward:
            return remote(
                src, up.at[step], up_send.at[step], up_recv.at[step],
                device(x, core, y, (z + hops) % NZ),
            )
        return remote(
            src, down.at[step], down_send.at[step], down_recv.at[step],
            device(x, core, y, (z + NZ - hops) % NZ),
        )

    def goes(plane):
        offset = (zl + NZL - zh + NZL - plane % NZL) % NZL
        return offset // 2, offset % 2, plane // NZL

    def y_copy(src, plane, index):
        reader, kind, half = goes(plane)
        return remote(
            src, home.at[kind, half * NY + y], y_send.at[index], y_recv.at[kind * 2 + half, y],
            device(x, core, reader, z),
        )

    def hand_on(src, plane, index):
        reader, kind, half = goes(plane)

        @pl.when(reader == y)
        def _():
            pltpu.make_async_copy(
                src, home.at[kind, half * NY + y], y_local.at[kind * 2 + half]
            ).start()

        @pl.when(reader != y)
        def _():
            y_copy(src, plane, index).start()

    def x_copy(kind, half, direction, piece):
        at = pl.ds(half * NY + piece * WIDE, WIDE)
        return remote(
            home.at[kind, at], near.at[direction, at],
            x_send.at[direction, kind * 2 + half, piece], x_recv.at[direction, half, piece],
            right if direction == 0 else left,
        )

    def forward(direction, half, piece):
        at = pl.ds(half * NY + piece * WIDE, WIDE)
        return remote(
            near.at[direction, at], across.at[0, at],
            f_send.at[direction, half, piece], f_recv.at[half, piece],
            right if direction == 0 else left,
        )

    def share(index, src, dst, half):
        return remote(
            src.at[group(half)], dst.at[group(half)], s_send.at[index, half], s_recv.at[index, half],
            sibling,
        )

    def share_home(kind, half):
        return share(0, home.at[kind], home.at[2], half)

    def share_near(direction, half):
        return share(1 + direction, near.at[direction], near.at[2 + direction], half)

    def share_across(half):
        return share(3, across.at[0], beyond.at[0], half)

    def sends(kind, direction):
        inner = (x < NX - 1) if direction == 0 else (x > 0)
        outer = (x == NX - 1) if direction == 0 else (x == 0)
        chosen = jnp.where(kind == direction, inner.astype(jnp.int32), outer.astype(jnp.int32))
        return chosen == 1

    def complete(plane):
        reader, kind, half = goes(plane)

        @pl.when(reader == y)
        def _():
            for v in others:
                remote(
                    own, home.at[kind, half * NY + v], y_send.at[0],
                    y_recv.at[kind * 2 + half, v], sibling,
                ).wait_recv()
            pltpu.make_async_copy(
                own, home.at[kind, half * NY + y], y_local.at[kind * 2 + half]
            ).wait()
            for direction in range(2):
                @pl.when(sends(kind, direction))
                def _():
                    for piece in range(PIECES):
                        x_copy(kind, half, direction, piece).start()

            @pl.when(kind == core)
            def _():
                share_home(kind, half).start()

    moves = ((0, 0, x < NX - 1), (0, 1, x == 2), (1, 1, x > 0), (1, 0, x == 1))
    kind_from = (jnp.where(x > 0, 0, 1), jnp.where(x < NX - 1, 1, 0))

    def pass_on(plane):
        reader, kind, half = goes(plane)
        for source in range(2):
            @pl.when((reader == y) & (kind == kind_from[source]))
            def _():
                for place_of in range(PIECES):
                    x_copy(kind, half, source, place_of).wait_recv()
                    for direction, piece, when in moves:
                        if direction == source and piece == place_of:
                            @pl.when(when)
                            def _():
                                forward(direction, half, piece).start()
                share_near(source, half).start()

    for hops in (2, 1):
        z_copy(own, hops, hops, True).start()
        z_copy(own, hops, hops, False).start()
    hand_on(own, z, 0)

    def at_lag(t, lag, act):
        @pl.when(t == lag)
        def _():
            act(z)

        @pl.when((t > lag) & (t < lag + FAR))
        def _():
            act((z + NZ - t + lag) % NZ)
            act((z + t - lag) % NZ)

        @pl.when(t == lag + FAR)
        def _():
            act((z + FAR) % NZ)

    def z_step(t):
        z_copy(own, t, 1, True).wait_recv()

        @pl.when((t % 2 == 0) & (t < FAR))
        def _():
            z_copy(up.at[t], t + 2, 2, True).start()
            z_copy(up.at[t], t + 1, 1, True).start()

        @pl.when(t < FAR)
        def _():
            z_copy(own, t, 1, False).wait_recv()

            @pl.when(t % 2 == 0)
            def _():
                @pl.when(t < FAR - 2)
                def _():
                    z_copy(down.at[t], t + 2, 2, False).start()

                z_copy(down.at[t], t + 1, 1, False).start()

        hand_on(up.at[t], (z + NZ - t) % NZ, t)

        @pl.when(t < FAR)
        def _():
            hand_on(down.at[t], (z + t) % NZ, FAR + t)

    def loop_body(t, carry):
        @pl.when(t <= FAR)
        def _():
            z_step(t)

        at_lag(t, Y_LAG, complete)
        at_lag(t, F_LAG, pass_on)
        return carry

    entries = STEPS * slots
    lanes = draft.shape[1]
    lane = lax.broadcasted_iota(jnp.int32, (1, lanes), 1)
    deep = lax.broadcasted_iota(jnp.int32, (lanes, lanes), 0)
    wide = lax.broadcasted_iota(jnp.int32, (lanes, lanes), 1)

    def upright(line):
        spread = jnp.where(deep == wide, jnp.broadcast_to(line, (lanes, lanes)), 0)
        return jnp.sum(spread, axis=1, keepdims=True)

    def falling(grid):
        return jnp.sum(grid, axis=0, keepdims=True)

    of_step = lane // slots
    slot = lane - of_step * slots
    limit = jnp.zeros_like(lane)
    for s in range(STEPS):
        limit = jnp.where(of_step == s, counts[0, s], limit)
    row_block = jnp.where(slot < limit, coords[0:1, :], BLOCKS)
    column_block = coords[1:2, :]
    key = of_step * (2 * BLOCKS) + row_block
    full = key * lanes + lane
    key_up = upright(key)
    rank_up = jnp.sum(
        (jnp.broadcast_to(full, (lanes, lanes)) < upright(full)).astype(jnp.int32),
        axis=1, keepdims=True,
    )
    hit = rank_up == wide
    order = falling(jnp.where(hit, deep, 0))
    spot_up = upright((column_block % NZH) * NY + column_block // NZH)
    ranked = falling(jnp.where(hit, key_up, 0))
    follows = (ranked == pltpu.roll(ranked, 1, 1)) & (lane > 0)
    goal = (lane // BLOCKS) * (2 * BLOCKS) + lane % BLOCKS
    upto = falling(((key_up <= goal) & (deep < entries)).astype(jnp.int32))
    some = falling(((key_up == goal) & (deep < entries)).astype(jnp.int32))
    draft[0:1, :] = order
    draft[1:2, :] = falling(jnp.where(hit, spot_up, 0))
    draft[2:3, :] = follows.astype(jnp.int32)
    draft[3:4, :] = jnp.where(some > 0, upto, 0)
    table_copy = pltpu.make_async_copy(draft, table, d_sem)

    def multiply(ref, index, step):
        for k in range(slots):
            e = step * slots + k
            product = jnp.dot(
                tiles[table[0, e]], ref[index, table[1, e]],
                preferred_element_type=jnp.float32,
            )
            if k > 0:
                product += jnp.where(table[2, e] == 1, sums[e], 0.0)
            sums[e + 1] = product

    def step_of(shared, rel):
        other = (rel * 2 + STEPS - 1 + core * 2) % STEPS
        return jnp.where(shared == 1, other, rel * 2)

    lax.fori_loop(1, FAR + Y_LAG + 1, loop_body, 0)
    sums[0] = jnp.zeros(sums.shape[1:], sums.dtype)
    table_copy.start()
    table_copy.wait()
    tile_copy.wait()
    weight_copy.wait()
    for half in range(2):
        share(0, home.at[0], home.at[2], half).wait_recv()

    def home_body(i, carry):
        multiply(home, i * 2, step_of(i, 0))
        return carry

    lax.fori_loop(0, 2, home_body, 0)
    lax.fori_loop(FAR + Y_LAG + 1, FAR + F_LAG + 1, loop_body, 0)
    for half in range(2):
        for direction in range(2):
            share_near(direction, half).wait_recv()

    def near_body(i, carry):
        multiply(near, i, step_of(i // 2, 1 + 2 * (i % 2)))
        return carry

    lax.fori_loop(0, 4, near_body, 0)
    for half in range(2):
        for piece in range(2):
            forward(0, half, piece).wait_recv()
        share_across(half).start()
    multiply(across, 0, step_of(0, 2))
    for half in range(2):
        share_across(half).wait_recv()
    multiply(beyond, 0, step_of(1, 2))

    def total(block):
        held = sums[table[3, block]]
        for step in range(1, STEPS):
            held += sums[table[3, block + step * BLOCKS]]
        return held

    def g_copy(turn, i):
        return remote(
            give.at[turn, i], got.at[turn, i], g_send.at[turn, i], g_recv.at[turn, i],
            device(x, core, others[i], z),
        )

    halves = (1 - zh, zh)
    for turn in range(2):
        for i in range(NY - 1):
            give[turn, i] = total(others[i] * NZH + halves[turn]).astype(give.dtype)
            g_copy(turn, i).start()
    to_partner = remote(z_give, z_got, z_send, z_recv, partner)
    for turn in range(2):
        hold[...] = total(y * NZH + halves[turn])
        for i in range(NY - 1):
            g_copy(turn, i).wait_recv()
        held = hold[...]
        for i in range(NY - 1):
            held += got[turn, i].astype(jnp.float32)
        if turn == 0:
            z_give[...] = held.astype(z_give.dtype)
            to_partner.start()
        else:
            hold[...] = held
    to_partner.wait()
    aggregated = (hold[...] + z_got[...].astype(jnp.float32)).astype(weight.dtype)
    product = jnp.dot(aggregated, weight[...], preferred_element_type=jnp.float32)
    out[...] = jnp.maximum(product, 0.0).astype(out.dtype)

    for turn in range(2):
        for i in range(NY - 1):
            g_copy(turn, i).wait_send()
    for half in range(2):
        share(0, home.at[0], home.at[2], half).wait_send()
        share_across(half).wait_send()
        for direction in range(2):
            share_near(direction, half).wait_send()
            for kind in range(2):
                @pl.when(sends(kind, direction))
                def _():
                    for piece in range(PIECES):
                        x_copy(kind, half, direction, piece).wait_send()
        for direction, piece, when in moves:
            @pl.when(when)
            def _():
                forward(direction, half, piece).wait_send()

    def hand_on_done(src, plane, index):
        @pl.when(goes(plane)[0] != y)
        def _():
            y_copy(src, plane, index).wait_send()

    hand_on_done(own, z, 0)

    def drain(t, carry):
        hand_on_done(up.at[t], (z + NZ - t) % NZ, t)
        z_copy(own, t, 1, True).wait_send()

        @pl.when(t < FAR)
        def _():
            hand_on_done(down.at[t], (z + t) % NZ, FAR + t)
            z_copy(own, t, 1, False).wait_send()

        return carry

    lax.fori_loop(1, FAR + 1, drain, 0)


def local(features, weight, tile_values, tile_coords, tile_counts):
    rows, width = features.shape
    slots = tile_values.shape[0] // STEPS
    coords = jnp.pad(tile_coords.T, ((0, 0), (0, LANES - tile_coords.shape[0])))
    dma = pltpu.SemaphoreType.DMA
    kind = features.dtype
    vmem = pl.BlockSpec(memory_space=pltpu.VMEM)
    hbm = pl.BlockSpec(memory_space=pl.ANY)
    return pl.pallas_call(
        functools.partial(layer_kernel, slots=slots),
        out_shape=jax.ShapeDtypeStruct((rows, weight.shape[1]), kind),
        in_specs=[
            pl.BlockSpec(memory_space=pltpu.SMEM), vmem, hbm, hbm, hbm,
        ],
        out_specs=vmem,
        scratch_shapes=[
            pltpu.VMEM((3, BLOCKS, rows, width), kind),
            pltpu.VMEM((4, BLOCKS, rows, width), kind),
            pltpu.VMEM((1, BLOCKS, rows, width), kind),
            pltpu.VMEM((1, BLOCKS, rows, width), kind),
            pltpu.VMEM((FAR + 1, rows, width), kind),
            pltpu.VMEM((FAR, rows, width), kind),
            pltpu.VMEM(tile_values.shape, kind),
            pltpu.VMEM((STEPS * slots + 1, rows, width), jnp.float32),
            pltpu.VMEM((2, NY - 1, rows, width), kind),
            pltpu.VMEM((2, NY - 1, rows, width), kind),
            pltpu.VMEM((rows, width), jnp.float32),
            pltpu.VMEM((rows, width), kind),
            pltpu.VMEM((rows, width), kind),
            pltpu.VMEM(weight.shape, kind),
            pltpu.VMEM((8, LANES), jnp.int32),
            pltpu.SMEM((8, LANES), jnp.int32),
            dma((FAR + 1,)), dma((FAR + 1,)), dma((FAR,)), dma((FAR,)),
            dma((NZ,)), dma((4, NY)), dma((4,)),
            dma((2, 4, PIECES)), dma((2, 2, PIECES)), dma((2, 2, PIECES)), dma((2, PIECES)),
            dma((4, 2)), dma((4, 2)),
            dma((2, NY - 1)), dma((2, NY - 1)), dma, dma, dma, dma, dma,
        ],
        compiler_params=pltpu.CompilerParams(
            collective_id=0, has_side_effects=True, vmem_limit_bytes=60 * 1024 * 1024
        ),
        name="layer",
    )(tile_counts, coords, features, weight, tile_values)


def solution(mesh):
    placed = (
        P(("loop", "rep"), None),
        P(),
        P(("loop", "rep"), None, None),
        P(("loop", "rep"), None),
        P(("loop", "rep"), None),
    )
    return jax.shard_map(
        local, mesh=mesh, in_specs=placed, out_specs=P(("loop", "rep"), None), check_vma=False
    )
```

```python
import functools

import jax
import jax.numpy as jnp
from jax import lax
from jax.experimental import pallas as pl
from jax.experimental.pallas import tpu as pltpu
from jax.sharding import PartitionSpec as P

MESH = pl.DeviceIdType.MESH
NX, NY, NZ, NC, NZH, NZL = 4, 4, 16, 2, 2, 8
STEPS = NX * NC
BLOCKS = NY * NZH
FAR = NZ // 2
PIECES = 2
PARTS = 2
LANES = 128
WIDE = NY // PIECES
Y_LAG, F_LAG, SYNC = 2, 6, 4


def place():
    l = lax.axis_index("loop")
    r = lax.axis_index("rep")
    zl, x, core = l // (NX * NC), (l // NC) % NX, l % NC
    y, zh = r // NZH, r % NZH
    return x, core, y, zh * NZL + zl


def device(x, core, y, z):
    return ((z % NZL) * (NX * NC) + x * NC + core, y * NZH + z // NZL)


def remote(src, dst, send, recv, target):
    return pltpu.make_async_remote_copy(
        src_ref=src, dst_ref=dst, send_sem=send, recv_sem=recv,
        device_id=target, device_id_type=MESH,
    )


def layer_kernel(
    counts_in, coords_in, own, weight_in, tiles_in, out,
    home, near, across, beyond, up, down, tiles, sums, give, got, hold, z_give, z_got,
    weight, draft, table, counts, coords, base,
    up_send, up_recv, down_send, down_recv, y_send, y_recv, y_local,
    x_send, x_recv, f_send, f_recv, s_send, s_recv,
    g_send, g_recv, z_send, z_recv, t_sem, w_sem, d_sem, c_sem, *, slots,
):
    x, core, y, z = place()
    zl, zh = z % NZL, z // NZL
    right = device((x + 1) % NX, core, y, z)
    left = device((x + NX - 1) % NX, core, y, z)
    above = device(x, core, y, (z + 1) % NZ)
    below = device(x, core, y, (z + NZ - 1) % NZ)
    sibling = device(x, 1 - core, y, z)
    partner = device(x, core, y, (z + NZL) % NZ)
    others = [(y + d) % NY for d in range(1, NY)]
    def group(half):
        return pl.ds(half * NY, NY)

    small_copies = (
        pltpu.make_async_copy(counts_in, counts, c_sem.at[0]),
        pltpu.make_async_copy(coords_in, coords, c_sem.at[1]),
    )
    tile_copy = pltpu.make_async_copy(tiles_in, tiles, t_sem)
    weight_copy = pltpu.make_async_copy(weight_in, weight, w_sem)

    barrier = pltpu.get_barrier_semaphore()
    friends = [right, left, above, below]
    friends += [device(x, core, v, z) for v in others]
    friends += [device(x, core, y, (z + d) % NZ) for d in (2, NZ - 2)]
    for friend in friends:
        pl.semaphore_signal(barrier, inc=1, device_id=friend, device_id_type=MESH)
    pl.semaphore_wait(barrier, len(friends) + core)
    pl.semaphore_signal(barrier, inc=1, device_id=sibling, device_id_type=MESH)

    def z_copy(src, step, hops, upward):
        if upward:
            return remote(
                src, up.at[step], up_send.at[step], up_recv.at[step],
                device(x, core, y, (z + hops) % NZ),
            )
        return remote(
            src, down.at[step], down_send.at[step], down_recv.at[step],
            device(x, core, y, (z + NZ - hops) % NZ),
        )

    def goes(plane):
        offset = (zl + NZL - zh + NZL - plane % NZL) % NZL
        return offset // 2, offset % 2, plane // NZL

    def y_copy(src, plane, index):
        reader, kind, half = goes(plane)
        return remote(
            src, home.at[kind, half * NY + y], y_send.at[index], y_recv.at[kind * 2 + half, y],
            device(x, core, reader, z),
        )

    def hand_on(src, plane, index):
        reader, kind, half = goes(plane)

        @pl.when(reader == y)
        def _():
            pltpu.make_async_copy(
                src, home.at[kind, half * NY + y], y_local.at[kind * 2 + half]
            ).start()

        @pl.when(reader != y)
        def _():
            y_copy(src, plane, index).start()

    def x_copy(kind, half, direction, piece):
        at = pl.ds(half * NY + piece * WIDE, WIDE)
        return remote(
            home.at[kind, at], near.at[direction, at],
            x_send.at[direction, kind * 2 + half, piece], x_recv.at[direction, half, piece],
            right if direction == 0 else left,
        )

    def forward(direction, half, piece):
        at = pl.ds(half * NY + piece * WIDE, WIDE)
        return remote(
            near.at[direction, at], across.at[0, at],
            f_send.at[direction, half, piece], f_recv.at[half, piece],
            right if direction == 0 else left,
        )

    def share(index, src, dst, half):
        return remote(
            src.at[group(half)], dst.at[group(half)], s_send.at[index, half], s_recv.at[index, half],
            sibling,
        )

    def share_home(kind, half):
        return share(0, home.at[kind], home.at[2], half)

    def share_near(direction, half):
        return share(1 + direction, near.at[direction], near.at[2 + direction], half)

    def share_across(half):
        return share(3, across.at[0], beyond.at[0], half)

    def sends(kind, direction):
        inner = (x < NX - 1) if direction == 0 else (x > 0)
        outer = (x == NX - 1) if direction == 0 else (x == 0)
        chosen = jnp.where(kind == direction, inner.astype(jnp.int32), outer.astype(jnp.int32))
        return chosen == 1

    def complete(plane):
        reader, kind, half = goes(plane)

        @pl.when(reader == y)
        def _():
            for v in others:
                remote(
                    own, home.at[kind, half * NY + v], y_send.at[0],
                    y_recv.at[kind * 2 + half, v], sibling,
                ).wait_recv()
            pltpu.make_async_copy(
                own, home.at[kind, half * NY + y], y_local.at[kind * 2 + half]
            ).wait()
            for direction in range(2):
                @pl.when(sends(kind, direction))
                def _():
                    for piece in range(PIECES):
                        x_copy(kind, half, direction, piece).start()

    def share_own(plane):
        reader, kind, half = goes(plane)

        @pl.when((reader == y) & (kind == core))
        def _():
            share_home(kind, half).start()

    moves = ((0, 0, x < NX - 1), (0, 1, x == 2), (1, 1, x > 0), (1, 0, x == 1))
    kind_from = (jnp.where(x > 0, 0, 1), jnp.where(x < NX - 1, 1, 0))

    def pass_on(plane):
        reader, kind, half = goes(plane)
        for source in range(2):
            @pl.when((reader == y) & (kind == kind_from[source]))
            def _():
                for place_of in range(PIECES):
                    x_copy(kind, half, source, place_of).wait_recv()
                    for direction, piece, when in moves:
                        if direction == source and piece == place_of:
                            @pl.when(when)
                            def _():
                                forward(direction, half, piece).start()
                share_near(source, half).start()

    for hops in (2, 1):
        z_copy(own, hops, hops, True).start()
        z_copy(own, hops, hops, False).start()
    hand_on(own, z, 0)
    for copy in small_copies:
        copy.start()
    tile_copy.start()
    weight_copy.start()

    def at_lag(t, lag, act):
        @pl.when(t == lag)
        def _():
            act(z)

        @pl.when((t > lag) & (t < lag + FAR))
        def _():
            act((z + NZ - t + lag) % NZ)
            act((z + t - lag) % NZ)

        @pl.when(t == lag + FAR)
        def _():
            act((z + FAR) % NZ)

    def z_step(t):
        z_copy(own, t, 1, True).wait_recv()

        @pl.when((t % 2 == 0) & (t < FAR))
        def _():
            z_copy(up.at[t], t + 2, 2, True).start()
            z_copy(up.at[t], t + 1, 1, True).start()

        @pl.when(t < FAR)
        def _():
            z_copy(own, t, 1, False).wait_recv()

            @pl.when(t % 2 == 0)
            def _():
                @pl.when(t < FAR - 2)
                def _():
                    z_copy(down.at[t], t + 2, 2, False).start()

                z_copy(down.at[t], t + 1, 1, False).start()

        hand_on(up.at[t], (z + NZ - t) % NZ, t)

        @pl.when(t < FAR)
        def _():
            hand_on(down.at[t], (z + t) % NZ, FAR + t)

    def loop_body(t, carry):
        @pl.when(t <= FAR)
        def _():
            z_step(t)

        at_lag(t, Y_LAG, complete)

        @pl.when(t == SYNC)
        def _():
            @pl.when(core == 0)
            def _():
                pl.semaphore_wait(barrier, 1)

            share_own(z)

            def earlier(d, nothing):
                share_own((z + d) % NZ)
                share_own((z + NZ - d) % NZ)
                return nothing

            lax.fori_loop(1, SYNC - Y_LAG + 1, earlier, 0)

        @pl.when(t > SYNC)
        def _():
            at_lag(t, Y_LAG, share_own)

        at_lag(t, F_LAG, pass_on)
        return carry

    rows = own.shape[0]
    entries = STEPS * slots
    lanes = draft.shape[1]
    lane = lax.broadcasted_iota(jnp.int32, (1, lanes), 1)
    deep = lax.broadcasted_iota(jnp.int32, (lanes, lanes), 0)
    wide = lax.broadcasted_iota(jnp.int32, (lanes, lanes), 1)

    def upright(line):
        spread = jnp.where(deep == wide, jnp.broadcast_to(line, (lanes, lanes)), 0)
        return jnp.sum(spread, axis=1, keepdims=True)

    def falling(grid):
        return jnp.sum(grid, axis=0, keepdims=True)

    for copy in small_copies:
        copy.wait()
    pad = jnp.zeros((2, lanes - entries), jnp.int32)
    places = jnp.concatenate([coords[...], pad], axis=1)
    of_step = lane // slots
    slot = lane - of_step * slots
    limit = jnp.zeros_like(lane)
    for s in range(STEPS):
        limit = jnp.where(of_step == s, counts[0, s], limit)
    row_block = jnp.where(slot < limit, places[0:1, :], BLOCKS)
    column_block = places[1:2, :]
    key = of_step * (2 * BLOCKS) + row_block
    full = key * lanes + lane
    key_up = upright(key)
    rank_up = jnp.sum(
        (jnp.broadcast_to(full, (lanes, lanes)) < upright(full)).astype(jnp.int32),
        axis=1, keepdims=True,
    )
    hit = rank_up == wide
    order = falling(jnp.where(hit, deep, 0))
    spot_up = upright((column_block % NZH) * NY + column_block // NZH)
    ranked = falling(jnp.where(hit, key_up, 0))
    follows = (ranked == pltpu.roll(ranked, 1, 1)) & (lane > 0)
    goal = (lane // BLOCKS) * (2 * BLOCKS) + lane % BLOCKS
    upto = falling(((key_up <= goal) & (deep < entries)).astype(jnp.int32))
    some = falling(((key_up == goal) & (deep < entries)).astype(jnp.int32))
    draft[0:1, :] = order
    draft[1:2, :] = falling(jnp.where(hit, spot_up, 0))
    draft[2:3, :] = follows.astype(jnp.int32)
    draft[3:4, :] = jnp.where(some > 0, upto, 0)
    table_copy = pltpu.make_async_copy(draft, table, d_sem)

    def multiply(ref, index, step):
        for k in range(slots):
            e = step * slots + k
            product = jnp.dot(
                tiles[table[0, e]], ref[index, table[1, e]],
                preferred_element_type=jnp.float32,
            )
            if k > 0:
                product += jnp.where(table[2, e] == 1, sums[e], 0.0)
            sums[e + 1] = product

    def step_of(shared, rel):
        other = (rel * 2 + STEPS - 1 + core * 2) % STEPS
        return shared * other + (1 - shared) * rel * 2

    lax.fori_loop(1, FAR + Y_LAG + 1, loop_body, 0)
    sums[0] = jnp.zeros(sums.shape[1:], sums.dtype)
    table_copy.start()
    table_copy.wait()
    tile_copy.wait()
    weight_copy.wait()
    for half in range(2):
        share(0, home.at[0], home.at[2], half).wait_recv()

    def home_body(i, carry):
        multiply(home, i * 2, step_of(i, 0))
        return carry

    lax.fori_loop(0, 2, home_body, 0)
    lax.fori_loop(FAR + Y_LAG + 1, FAR + F_LAG + 1, loop_body, 0)
    for half in range(2):
        for direction in range(2):
            share_near(direction, half).wait_recv()

    def near_body(i, carry):
        multiply(near, i, step_of(i // 2, 1 + 2 * (i % 2)))
        return carry

    lax.fori_loop(0, 4, near_body, 0)
    early = [step_of(shared, rel) for shared in range(2) for rel in (0, 1, 3)]
    late = [step_of(shared, 2) for shared in range(2)]

    def base_body(block, carry):
        held = sums[table[3, block + early[0] * BLOCKS]]
        for step in early[1:]:
            held += sums[table[3, block + step * BLOCKS]]
        base[block] = held
        return carry

    lax.fori_loop(0, BLOCKS, base_body, 0)
    for half in range(2):
        for piece in range(2):
            forward(0, half, piece).wait_recv()
        share_across(half).start()
    multiply(across, 0, step_of(0, 2))
    for half in range(2):
        share_across(half).wait_recv()
    multiply(beyond, 0, step_of(1, 2))

    span = rows // PARTS

    def total(block, at):
        held = base[block, at]
        for step in late:
            held += sums[table[3, block + step * BLOCKS], at]
        return held

    def g_copy(turn, i, p):
        at = pl.ds(p * span, span)
        return remote(
            give.at[turn, i, at], got.at[turn, i, at], g_send.at[turn, i, p],
            g_recv.at[turn, i, p], device(x, core, others[i], z),
        )

    def across_z(p):
        at = pl.ds(p * span, span)
        return remote(z_give.at[at], z_got.at[at], z_send.at[p], z_recv.at[p], partner)

    halves = (1 - zh, zh)
    cuts = [pl.ds(p * span, span) for p in range(PARTS)]
    for turn in range(2):
        for p in range(PARTS):
            for i in range(NY - 1):
                give[turn, i, cuts[p]] = total(
                    others[i] * NZH + halves[turn], cuts[p]
                ).astype(give.dtype)
                g_copy(turn, i, p).start()

    def gathered(turn, p):
        held = total(y * NZH + halves[turn], cuts[p])
        for i in range(NY - 1):
            g_copy(turn, i, p).wait_recv()
        for i in range(NY - 1):
            held += got[turn, i, cuts[p]].astype(jnp.float32)
        return held

    for p in range(PARTS):
        z_give[cuts[p]] = gathered(0, p).astype(z_give.dtype)
        across_z(p).start()
    for p in range(PARTS):
        hold[cuts[p]] = gathered(1, p)
    for p in range(PARTS):
        across_z(p).wait()
        aggregated = (hold[cuts[p]] + z_got[cuts[p]].astype(jnp.float32)).astype(weight.dtype)
        product = jnp.dot(aggregated, weight[...], preferred_element_type=jnp.float32)
        out[cuts[p]] = jnp.maximum(product, 0.0).astype(out.dtype)

    for turn in range(2):
        for i in range(NY - 1):
            for p in range(PARTS):
                g_copy(turn, i, p).wait_send()
    for half in range(2):
        share(0, home.at[0], home.at[2], half).wait_send()
        share_across(half).wait_send()
        for direction in range(2):
            share_near(direction, half).wait_send()
            for kind in range(2):
                @pl.when(sends(kind, direction))
                def _():
                    for piece in range(PIECES):
                        x_copy(kind, half, direction, piece).wait_send()
        for direction, piece, when in moves:
            @pl.when(when)
            def _():
                forward(direction, half, piece).wait_send()

    def hand_on_done(src, plane, index):
        @pl.when(goes(plane)[0] != y)
        def _():
            y_copy(src, plane, index).wait_send()

    hand_on_done(own, z, 0)

    def drain(t, carry):
        hand_on_done(up.at[t], (z + NZ - t) % NZ, t)
        z_copy(own, t, 1, True).wait_send()

        @pl.when(t < FAR)
        def _():
            hand_on_done(down.at[t], (z + t) % NZ, FAR + t)
            z_copy(own, t, 1, False).wait_send()

        return carry

    lax.fori_loop(1, FAR + 1, drain, 0)


def local(features, weight, tile_values, tile_coords, tile_counts):
    rows, width = features.shape
    slots = tile_values.shape[0] // STEPS
    dma = pltpu.SemaphoreType.DMA
    kind = features.dtype
    vmem = pl.BlockSpec(memory_space=pltpu.VMEM)
    hbm = pl.BlockSpec(memory_space=pltpu.HBM)
    return pl.pallas_call(
        functools.partial(layer_kernel, slots=slots),
        out_shape=jax.ShapeDtypeStruct((rows, weight.shape[1]), kind),
        in_specs=[
            hbm, hbm, hbm, hbm, hbm,
        ],
        out_specs=vmem,
        scratch_shapes=[
            pltpu.VMEM((3, BLOCKS, rows, width), kind),
            pltpu.VMEM((4, BLOCKS, rows, width), kind),
            pltpu.VMEM((1, BLOCKS, rows, width), kind),
            pltpu.VMEM((1, BLOCKS, rows, width), kind),
            pltpu.VMEM((FAR + 1, rows, width), kind),
            pltpu.VMEM((FAR, rows, width), kind),
            pltpu.VMEM(tile_values.shape, kind),
            pltpu.VMEM((STEPS * slots + 1, rows, width), jnp.float32),
            pltpu.VMEM((2, NY - 1, rows, width), kind),
            pltpu.VMEM((2, NY - 1, rows, width), kind),
            pltpu.VMEM((rows, width), jnp.float32),
            pltpu.VMEM((rows, width), kind),
            pltpu.VMEM((rows, width), kind),
            pltpu.VMEM(weight.shape, kind),
            pltpu.VMEM((8, LANES), jnp.int32),
            pltpu.SMEM((8, LANES), jnp.int32),
            pltpu.SMEM(tile_counts.shape, jnp.int32),
            pltpu.VMEM(tile_coords.T.shape, jnp.int32),
            pltpu.VMEM((BLOCKS, rows, width), jnp.float32),
            dma((FAR + 1,)), dma((FAR + 1,)), dma((FAR,)), dma((FAR,)),
            dma((NZ,)), dma((4, NY)), dma((4,)),
            dma((2, 4, PIECES)), dma((2, 2, PIECES)), dma((2, 2, PIECES)), dma((2, PIECES)),
            dma((4, 2)), dma((4, 2)),
            dma((2, NY - 1, PARTS)), dma((2, NY - 1, PARTS)), dma((PARTS,)), dma((PARTS,)),
            dma, dma, dma, dma((2,)),
        ],
        compiler_params=pltpu.CompilerParams(
            collective_id=0, has_side_effects=True, vmem_limit_bytes=60 * 1024 * 1024
        ),
        name="layer",
    )(tile_counts, tile_coords.T, features, weight, tile_values)


def solution(mesh):
    placed = (
        P(("loop", "rep"), None),
        P(),
        P(("loop", "rep"), None, None),
        P(("loop", "rep"), None),
        P(("loop", "rep"), None),
    )
    return jax.shard_map(
        local, mesh=mesh, in_specs=placed, out_specs=P(("loop", "rep"), None), check_vma=False
    )
```

```python
import functools

import jax
import jax.numpy as jnp
from jax import lax
from jax.experimental import pallas as pl
from jax.experimental.pallas import tpu as pltpu
from jax.sharding import PartitionSpec as P

MESH = pl.DeviceIdType.MESH
NX, NY, NZ, NC, NZH, NZL = 4, 4, 16, 2, 2, 8
STEPS = NX * NC
BLOCKS = NY * NZH
FAR = NZ // 2
PIECES = 2
CHUNKS = 1
PARTS = 2
LANES = 128
WIDE = NY // PIECES
Y_LAG, F_LAG, SYNC = 2, 6, 4


def place():
    l = lax.axis_index("loop")
    r = lax.axis_index("rep")
    zl, x, core = l // (NX * NC), (l // NC) % NX, l % NC
    y, zh = r // NZH, r % NZH
    return x, core, y, zh * NZL + zl


def device(x, core, y, z):
    return ((z % NZL) * (NX * NC) + x * NC + core, y * NZH + z // NZL)


def remote(src, dst, send, recv, target):
    return pltpu.make_async_remote_copy(
        src_ref=src, dst_ref=dst, send_sem=send, recv_sem=recv,
        device_id=target, device_id_type=MESH,
    )


def layer_kernel(
    counts_in, coords_in, own, weight_in, tiles_in, out,
    home, near, across, beyond, up, down, tiles, sums, give, got, hold, z_give, z_got,
    weight, draft, table, counts, coords, base,
    up_send, up_recv, down_send, down_recv, y_send, y_recv, y_local,
    x_send, x_recv, f_send, f_recv, s_send, s_recv,
    g_send, g_recv, z_send, z_recv, t_sem, w_sem, d_sem, c_sem, *, slots,
):
    x, core, y, z = place()
    zl, zh = z % NZL, z // NZL
    right = device((x + 1) % NX, core, y, z)
    left = device((x + NX - 1) % NX, core, y, z)
    above = device(x, core, y, (z + 1) % NZ)
    below = device(x, core, y, (z + NZ - 1) % NZ)
    sibling = device(x, 1 - core, y, z)
    partner = device(x, core, y, (z + NZL) % NZ)
    others = [(y + d) % NY for d in range(1, NY)]
    def group(half):
        return pl.ds(half * NY, NY)

    small_copies = (
        pltpu.make_async_copy(counts_in, counts, c_sem.at[0]),
        pltpu.make_async_copy(coords_in, coords, c_sem.at[1]),
    )
    tile_copy = pltpu.make_async_copy(tiles_in, tiles, t_sem)
    weight_copy = pltpu.make_async_copy(weight_in, weight, w_sem)

    barrier = pltpu.get_barrier_semaphore()
    friends = [right, left, above, below]
    friends += [device(x, core, v, z) for v in others]
    friends += [device(x, core, y, (z + d) % NZ) for d in (2, NZ - 2)]
    for friend in friends:
        pl.semaphore_signal(barrier, inc=1, device_id=friend, device_id_type=MESH)
    pl.semaphore_wait(barrier, len(friends) + core)
    pl.semaphore_signal(barrier, inc=1, device_id=sibling, device_id_type=MESH)

    grain = own.shape[0] // CHUNKS

    def z_copy(src, step, hops, upward, chunk):
        at = pl.ds(chunk * grain, grain)
        if upward:
            return remote(
                src.at[at], up.at[step, at], up_send.at[step, chunk], up_recv.at[step, chunk],
                device(x, core, y, (z + hops) % NZ),
            )
        return remote(
            src.at[at], down.at[step, at], down_send.at[step, chunk], down_recv.at[step, chunk],
            device(x, core, y, (z + NZ - hops) % NZ),
        )

    def goes(plane):
        offset = (zl + NZL - zh + NZL - plane % NZL) % NZL
        return offset // 2, offset % 2, plane // NZL

    def y_copy(src, plane, index):
        reader, kind, half = goes(plane)
        return remote(
            src, home.at[kind, half * NY + y], y_send.at[index], y_recv.at[kind * 2 + half, y],
            device(x, core, reader, z),
        )

    def hand_on(src, plane, index):
        reader, kind, half = goes(plane)

        @pl.when(reader == y)
        def _():
            pltpu.make_async_copy(
                src, home.at[kind, half * NY + y], y_local.at[kind * 2 + half]
            ).start()

        @pl.when(reader != y)
        def _():
            y_copy(src, plane, index).start()

    def x_copy(kind, half, direction, piece):
        at = pl.ds(half * NY + piece * WIDE, WIDE)
        return remote(
            home.at[kind, at], near.at[direction, at],
            x_send.at[direction, kind * 2 + half, piece], x_recv.at[direction, half, piece],
            right if direction == 0 else left,
        )

    def forward(direction, half, piece):
        at = pl.ds(half * NY + piece * WIDE, WIDE)
        return remote(
            near.at[direction, at], across.at[0, at],
            f_send.at[direction, half, piece], f_recv.at[half, piece],
            right if direction == 0 else left,
        )

    def share(index, src, dst, half):
        return remote(
            src.at[group(half)], dst.at[group(half)], s_send.at[index, half], s_recv.at[index, half],
            sibling,
        )

    def share_home(kind, half):
        return share(0, home.at[kind], home.at[2], half)

    def share_near(direction, half):
        return share(1 + direction, near.at[direction], near.at[2 + direction], half)

    def share_across(half):
        return share(3, across.at[0], beyond.at[0], half)

    def sends(kind, direction):
        inner = (x < NX - 1) if direction == 0 else (x > 0)
        outer = (x == NX - 1) if direction == 0 else (x == 0)
        chosen = jnp.where(kind == direction, inner.astype(jnp.int32), outer.astype(jnp.int32))
        return chosen == 1

    def complete(plane):
        reader, kind, half = goes(plane)

        @pl.when(reader == y)
        def _():
            for v in others:
                remote(
                    own, home.at[kind, half * NY + v], y_send.at[0],
                    y_recv.at[kind * 2 + half, v], sibling,
                ).wait_recv()
            pltpu.make_async_copy(
                own, home.at[kind, half * NY + y], y_local.at[kind * 2 + half]
            ).wait()
            for direction in range(2):
                @pl.when(sends(kind, direction))
                def _():
                    for piece in range(PIECES):
                        x_copy(kind, half, direction, piece).start()

    def share_own(plane):
        reader, kind, half = goes(plane)

        @pl.when((reader == y) & (kind == core))
        def _():
            share_home(kind, half).start()

    moves = ((0, 0, x < NX - 1), (0, 1, x == 2), (1, 1, x > 0), (1, 0, x == 1))
    kind_from = (jnp.where(x > 0, 0, 1), jnp.where(x < NX - 1, 1, 0))

    def pass_on(plane):
        reader, kind, half = goes(plane)
        for source in range(2):
            @pl.when((reader == y) & (kind == kind_from[source]))
            def _():
                for place_of in range(PIECES):
                    x_copy(kind, half, source, place_of).wait_recv()
                    for direction, piece, when in moves:
                        if direction == source and piece == place_of:
                            @pl.when(when)
                            def _():
                                forward(direction, half, piece).start()
                share_near(source, half).start()

    for hops in (2, 1):
        for chunk in range(CHUNKS):
            z_copy(own, hops, hops, True, chunk).start()
            z_copy(own, hops, hops, False, chunk).start()
    hand_on(own, z, 0)
    for copy in small_copies:
        copy.start()
    tile_copy.start()
    weight_copy.start()

    def distance(q):
        return q + 2 * (q % 2) - 1

    def at_lag(t, lag, act):
        q = t - lag
        d = distance(jnp.maximum(q, 1))

        @pl.when(q == 0)
        def _():
            act(z)

        @pl.when((q > 0) & (q <= FAR))
        def _():
            act((z + NZ - d) % NZ)

            @pl.when(d < FAR)
            def _():
                act((z + d) % NZ)

    def z_step(t):
        d = distance(t)
        even = d % 2 == 0
        for chunk in range(CHUNKS):
            z_copy(own, d, 1, True, chunk).wait_recv()

            @pl.when(even & (d < FAR))
            def _():
                z_copy(up.at[d], d + 2, 2, True, chunk).start()

            @pl.when(d < FAR)
            def _():
                z_copy(own, d, 1, False, chunk).wait_recv()

                @pl.when(even & (d < FAR - 2))
                def _():
                    z_copy(down.at[d], d + 2, 2, False, chunk).start()

        @pl.when(even & (d < FAR))
        def _():
            for chunk in range(CHUNKS):
                z_copy(up.at[d], d + 1, 1, True, chunk).start()
                z_copy(down.at[d], d + 1, 1, False, chunk).start()

        hand_on(up.at[d], (z + NZ - d) % NZ, d)

        @pl.when(d < FAR)
        def _():
            hand_on(down.at[d], (z + d) % NZ, FAR + d)

    def loop_body(t, carry):
        @pl.when(t <= FAR)
        def _():
            z_step(t)

        at_lag(t, Y_LAG, complete)

        @pl.when(t == SYNC)
        def _():
            @pl.when(core == 0)
            def _():
                pl.semaphore_wait(barrier, 1)

            share_own(z)

            def earlier(d, nothing):
                share_own((z + d) % NZ)
                share_own((z + NZ - d) % NZ)
                return nothing

            lax.fori_loop(1, SYNC - Y_LAG + 1, earlier, 0)

        @pl.when(t > SYNC)
        def _():
            at_lag(t, Y_LAG, share_own)

        at_lag(t, F_LAG, pass_on)
        return carry

    rows = own.shape[0]
    entries = STEPS * slots
    lanes = draft.shape[1]
    lane = lax.broadcasted_iota(jnp.int32, (1, lanes), 1)
    deep = lax.broadcasted_iota(jnp.int32, (lanes, lanes), 0)
    wide = lax.broadcasted_iota(jnp.int32, (lanes, lanes), 1)

    def upright(line):
        spread = jnp.where(deep == wide, jnp.broadcast_to(line, (lanes, lanes)), 0)
        return jnp.sum(spread, axis=1, keepdims=True)

    def falling(grid):
        return jnp.sum(grid, axis=0, keepdims=True)

    for copy in small_copies:
        copy.wait()
    pad = jnp.zeros((2, lanes - entries), jnp.int32)
    places = jnp.concatenate([coords[...], pad], axis=1)
    of_step = lane // slots
    slot = lane - of_step * slots
    limit = jnp.zeros_like(lane)
    for s in range(STEPS):
        limit = jnp.where(of_step == s, counts[0, s], limit)
    row_block = jnp.where(slot < limit, places[0:1, :], BLOCKS)
    column_block = places[1:2, :]
    key = of_step * (2 * BLOCKS) + row_block
    full = key * lanes + lane
    key_up = upright(key)
    rank_up = jnp.sum(
        (jnp.broadcast_to(full, (lanes, lanes)) < upright(full)).astype(jnp.int32),
        axis=1, keepdims=True,
    )
    hit = rank_up == wide
    order = falling(jnp.where(hit, deep, 0))
    spot_up = upright((column_block % NZH) * NY + column_block // NZH)
    ranked = falling(jnp.where(hit, key_up, 0))
    follows = (ranked == pltpu.roll(ranked, 1, 1)) & (lane > 0)
    goal = (lane // BLOCKS) * (2 * BLOCKS) + lane % BLOCKS
    upto = falling(((key_up <= goal) & (deep < entries)).astype(jnp.int32))
    some = falling(((key_up == goal) & (deep < entries)).astype(jnp.int32))
    draft[0:1, :] = order
    draft[1:2, :] = falling(jnp.where(hit, spot_up, 0))
    draft[2:3, :] = follows.astype(jnp.int32)
    draft[3:4, :] = jnp.where(some > 0, upto, 0)
    table_copy = pltpu.make_async_copy(draft, table, d_sem)

    def multiply(ref, index, step):
        for k in range(slots):
            e = step * slots + k
            product = jnp.dot(
                tiles[table[0, e]], ref[index, table[1, e]],
                preferred_element_type=jnp.float32,
            )
            if k > 0:
                product += jnp.where(table[2, e] == 1, sums[e], 0.0)
            sums[e + 1] = product

    def step_of(shared, rel):
        other = (rel * 2 + STEPS - 1 + core * 2) % STEPS
        return shared * other + (1 - shared) * rel * 2

    lax.fori_loop(1, FAR + Y_LAG + 1, loop_body, 0)
    sums[0] = jnp.zeros(sums.shape[1:], sums.dtype)
    table_copy.start()
    table_copy.wait()
    tile_copy.wait()
    weight_copy.wait()
    for half in range(2):
        share(0, home.at[0], home.at[2], half).wait_recv()

    def home_body(i, carry):
        multiply(home, i * 2, step_of(i, 0))
        return carry

    lax.fori_loop(0, 2, home_body, 0)
    lax.fori_loop(FAR + Y_LAG + 1, FAR + F_LAG + 1, loop_body, 0)
    for half in range(2):
        for direction in range(2):
            share_near(direction, half).wait_recv()

    def near_body(i, carry):
        multiply(near, i, step_of(i // 2, 1 + 2 * (i % 2)))
        return carry

    lax.fori_loop(0, 4, near_body, 0)
    early = [step_of(shared, rel) for shared in range(2) for rel in (0, 1, 3)]
    late = [step_of(shared, 2) for shared in range(2)]

    def base_body(block, carry):
        held = sums[table[3, block + early[0] * BLOCKS]]
        for step in early[1:]:
            held += sums[table[3, block + step * BLOCKS]]
        base[block] = held
        return carry

    lax.fori_loop(0, BLOCKS, base_body, 0)
    for half in range(2):
        for piece in range(2):
            forward(0, half, piece).wait_recv()
        share_across(half).start()
    multiply(across, 0, step_of(0, 2))
    for half in range(2):
        share_across(half).wait_recv()
    multiply(beyond, 0, step_of(1, 2))

    span = rows // PARTS

    def total(block, at):
        held = base[block, at]
        for step in late:
            held += sums[table[3, block + step * BLOCKS], at]
        return held

    def g_copy(turn, i, p):
        at = pl.ds(p * span, span)
        return remote(
            give.at[turn, i, at], got.at[turn, i, at], g_send.at[turn, i, p],
            g_recv.at[turn, i, p], device(x, core, others[i], z),
        )

    def across_z(p):
        at = pl.ds(p * span, span)
        return remote(z_give.at[at], z_got.at[at], z_send.at[p], z_recv.at[p], partner)

    halves = (1 - zh, zh)
    cuts = [pl.ds(p * span, span) for p in range(PARTS)]
    for turn in range(2):
        for p in range(PARTS):
            for i in range(NY - 1):
                give[turn, i, cuts[p]] = total(
                    others[i] * NZH + halves[turn], cuts[p]
                ).astype(give.dtype)
                g_copy(turn, i, p).start()

    def gathered(turn, p):
        held = total(y * NZH + halves[turn], cuts[p])
        for i in range(NY - 1):
            g_copy(turn, i, p).wait_recv()
        for i in range(NY - 1):
            held += got[turn, i, cuts[p]].astype(jnp.float32)
        return held

    for p in range(PARTS):
        z_give[cuts[p]] = gathered(0, p).astype(z_give.dtype)
        across_z(p).start()
    for p in range(PARTS):
        hold[cuts[p]] = gathered(1, p)
    for p in range(PARTS):
        across_z(p).wait()
        aggregated = (hold[cuts[p]] + z_got[cuts[p]].astype(jnp.float32)).astype(weight.dtype)
        product = jnp.dot(aggregated, weight[...], preferred_element_type=jnp.float32)
        out[cuts[p]] = jnp.maximum(product, 0.0).astype(out.dtype)

    for turn in range(2):
        for i in range(NY - 1):
            for p in range(PARTS):
                g_copy(turn, i, p).wait_send()
    for half in range(2):
        share(0, home.at[0], home.at[2], half).wait_send()
        share_across(half).wait_send()
        for direction in range(2):
            share_near(direction, half).wait_send()
            for kind in range(2):
                @pl.when(sends(kind, direction))
                def _():
                    for piece in range(PIECES):
                        x_copy(kind, half, direction, piece).wait_send()
        for direction, piece, when in moves:
            @pl.when(when)
            def _():
                forward(direction, half, piece).wait_send()

    def hand_on_done(src, plane, index):
        @pl.when(goes(plane)[0] != y)
        def _():
            y_copy(src, plane, index).wait_send()

    hand_on_done(own, z, 0)

    def drain(t, carry):
        hand_on_done(up.at[t], (z + NZ - t) % NZ, t)
        for chunk in range(CHUNKS):
            z_copy(own, t, 1, True, chunk).wait_send()

        @pl.when(t < FAR)
        def _():
            hand_on_done(down.at[t], (z + t) % NZ, FAR + t)
            for chunk in range(CHUNKS):
                z_copy(own, t, 1, False, chunk).wait_send()

        return carry

    lax.fori_loop(1, FAR + 1, drain, 0)


def local(features, weight, tile_values, tile_coords, tile_counts):
    rows, width = features.shape
    slots = tile_values.shape[0] // STEPS
    dma = pltpu.SemaphoreType.DMA
    kind = features.dtype
    vmem = pl.BlockSpec(memory_space=pltpu.VMEM)
    hbm = pl.BlockSpec(memory_space=pltpu.HBM)
    return pl.pallas_call(
        functools.partial(layer_kernel, slots=slots),
        out_shape=jax.ShapeDtypeStruct((rows, weight.shape[1]), kind),
        in_specs=[
            hbm, hbm, hbm, hbm, hbm,
        ],
        out_specs=vmem,
        scratch_shapes=[
            pltpu.VMEM((3, BLOCKS, rows, width), kind),
            pltpu.VMEM((4, BLOCKS, rows, width), kind),
            pltpu.VMEM((1, BLOCKS, rows, width), kind),
            pltpu.VMEM((1, BLOCKS, rows, width), kind),
            pltpu.VMEM((FAR + 1, rows, width), kind),
            pltpu.VMEM((FAR, rows, width), kind),
            pltpu.VMEM(tile_values.shape, kind),
            pltpu.VMEM((STEPS * slots + 1, rows, width), jnp.float32),
            pltpu.VMEM((2, NY - 1, rows, width), kind),
            pltpu.VMEM((2, NY - 1, rows, width), kind),
            pltpu.VMEM((rows, width), jnp.float32),
            pltpu.VMEM((rows, width), kind),
            pltpu.VMEM((rows, width), kind),
            pltpu.VMEM(weight.shape, kind),
            pltpu.VMEM((8, LANES), jnp.int32),
            pltpu.SMEM((8, LANES), jnp.int32),
            pltpu.SMEM(tile_counts.shape, jnp.int32),
            pltpu.VMEM(tile_coords.T.shape, jnp.int32),
            pltpu.VMEM((BLOCKS, rows, width), jnp.float32),
            dma((FAR + 1, CHUNKS)), dma((FAR + 1, CHUNKS)), dma((FAR, CHUNKS)), dma((FAR, CHUNKS)),
            dma((NZ,)), dma((4, NY)), dma((4,)),
            dma((2, 4, PIECES)), dma((2, 2, PIECES)), dma((2, 2, PIECES)), dma((2, PIECES)),
            dma((4, 2)), dma((4, 2)),
            dma((2, NY - 1, PARTS)), dma((2, NY - 1, PARTS)), dma((PARTS,)), dma((PARTS,)),
            dma, dma, dma, dma((2,)),
        ],
        compiler_params=pltpu.CompilerParams(
            collective_id=0, has_side_effects=True, vmem_limit_bytes=60 * 1024 * 1024
        ),
        name="layer",
    )(tile_counts, tile_coords.T, features, weight, tile_values)


def solution(mesh):
    placed = (
        P(("loop", "rep"), None),
        P(),
        P(("loop", "rep"), None, None),
        P(("loop", "rep"), None),
        P(("loop", "rep"), None),
    )
    return jax.shard_map(
        local, mesh=mesh, in_specs=placed, out_specs=P(("loop", "rep"), None), check_vma=False
    )
```

```python
import functools

import jax
import jax.numpy as jnp
from jax import lax
from jax.experimental import pallas as pl
from jax.experimental.pallas import tpu as pltpu
from jax.sharding import PartitionSpec as P

MESH = pl.DeviceIdType.MESH
NX, NY, NZ, NC, NZH, NZL = 4, 4, 16, 2, 2, 8
STEPS = NX * NC
BLOCKS = NY * NZH
FAR = NZ // 2
PIECES = 2
CHUNKS = 1
PARTS = 2
LANES = 128
WIDE = NY // PIECES
Y_LAG, F_LAG, SYNC = 2, 6, 4


def place():
    l = lax.axis_index("loop")
    r = lax.axis_index("rep")
    zl, x, core = l // (NX * NC), (l // NC) % NX, l % NC
    y, zh = r // NZH, r % NZH
    return x, core, y, zh * NZL + zl


def device(x, core, y, z):
    return ((z % NZL) * (NX * NC) + x * NC + core, y * NZH + z // NZL)


def remote(src, dst, send, recv, target):
    return pltpu.make_async_remote_copy(
        src_ref=src, dst_ref=dst, send_sem=send, recv_sem=recv,
        device_id=target, device_id_type=MESH,
    )


def layer_kernel(
    counts_in, coords_in, own, weight_in, tiles_in, out,
    home, near, across, beyond, up, down, tiles, sums, give, got, hold, z_give, z_got,
    weight, draft, table, counts, coords, base,
    up_send, up_recv, down_send, down_recv, y_send, y_recv, y_local,
    x_send, x_recv, f_send, f_recv, s_send, s_recv,
    g_send, g_recv, z_send, z_recv, t_sem, w_sem, d_sem, c_sem, *, slots,
):
    x, core, y, z = place()
    zl, zh = z % NZL, z // NZL
    right = device((x + 1) % NX, core, y, z)
    left = device((x + NX - 1) % NX, core, y, z)
    above = device(x, core, y, (z + 1) % NZ)
    below = device(x, core, y, (z + NZ - 1) % NZ)
    sibling = device(x, 1 - core, y, z)
    partner = device(x, core, y, (z + NZL) % NZ)
    others = [(y + d) % NY for d in range(1, NY)]
    def group(half):
        return pl.ds(half * NY, NY)

    small_copies = (
        pltpu.make_async_copy(counts_in, counts, c_sem.at[0]),
        pltpu.make_async_copy(coords_in, coords, c_sem.at[1]),
    )
    tile_copy = pltpu.make_async_copy(tiles_in, tiles, t_sem)
    weight_copy = pltpu.make_async_copy(weight_in, weight, w_sem)

    barrier = pltpu.get_barrier_semaphore()
    friends = [right, left, above, below]
    friends += [device(x, core, v, z) for v in others]
    friends += [device(x, core, y, (z + d) % NZ) for d in (2, NZ - 2)]
    for friend in friends:
        pl.semaphore_signal(barrier, inc=1, device_id=friend, device_id_type=MESH)
    pl.semaphore_wait(barrier, len(friends) + core)
    pl.semaphore_signal(barrier, inc=1, device_id=sibling, device_id_type=MESH)

    grain = own.shape[0] // CHUNKS

    def z_copy(src, step, hops, upward, chunk):
        at = pl.ds(chunk * grain, grain)
        if upward:
            return remote(
                src.at[at], up.at[step, at], up_send.at[step, chunk], up_recv.at[step, chunk],
                device(x, core, y, (z + hops) % NZ),
            )
        return remote(
            src.at[at], down.at[step, at], down_send.at[step, chunk], down_recv.at[step, chunk],
            device(x, core, y, (z + NZ - hops) % NZ),
        )

    def goes(plane):
        offset = (zl + NZL - zh + NZL - plane % NZL) % NZL
        return offset // 2, offset % 2, plane // NZL

    def y_copy(src, plane, index):
        reader, kind, half = goes(plane)
        return remote(
            src, home.at[kind, half * NY + y], y_send.at[index], y_recv.at[kind * 2 + half, y],
            device(x, core, reader, z),
        )

    def hand_on(src, plane, index):
        reader, kind, half = goes(plane)

        @pl.when(reader == y)
        def _():
            pltpu.make_async_copy(
                src, home.at[kind, half * NY + y], y_local.at[kind * 2 + half]
            ).start()

        @pl.when(reader != y)
        def _():
            y_copy(src, plane, index).start()

    def x_copy(kind, half, direction, piece):
        at = pl.ds(half * NY + piece * WIDE, WIDE)
        return remote(
            home.at[kind, at], near.at[direction, at],
            x_send.at[direction, kind * 2 + half, piece], x_recv.at[direction, half, piece],
            right if direction == 0 else left,
        )

    def forward(direction, half, piece):
        at = pl.ds(half * NY + piece * WIDE, WIDE)
        return remote(
            near.at[direction, at], across.at[0, at],
            f_send.at[direction, half, piece], f_recv.at[half, piece],
            right if direction == 0 else left,
        )

    def share(index, src, dst, half):
        return remote(
            src.at[group(half)], dst.at[group(half)], s_send.at[index, half], s_recv.at[index, half],
            sibling,
        )

    def share_home(kind, half):
        return share(0, home.at[kind], home.at[2], half)

    def share_near(direction, half):
        return share(1 + direction, near.at[direction], near.at[2 + direction], half)

    def share_across(half, piece):
        at = pl.ds(half * NY + piece * WIDE, WIDE)
        return remote(
            across.at[0, at], beyond.at[0, at], s_send.at[3 + piece, half],
            s_recv.at[3 + piece, half], sibling,
        )

    def sends(kind, direction):
        inner = (x < NX - 1) if direction == 0 else (x > 0)
        outer = (x == NX - 1) if direction == 0 else (x == 0)
        chosen = jnp.where(kind == direction, inner.astype(jnp.int32), outer.astype(jnp.int32))
        return chosen == 1

    def complete(plane):
        reader, kind, half = goes(plane)

        @pl.when(reader == y)
        def _():
            for v in others:
                remote(
                    own, home.at[kind, half * NY + v], y_send.at[0],
                    y_recv.at[kind * 2 + half, v], sibling,
                ).wait_recv()
            pltpu.make_async_copy(
                own, home.at[kind, half * NY + y], y_local.at[kind * 2 + half]
            ).wait()
            for direction in range(2):
                @pl.when(sends(kind, direction))
                def _():
                    for piece in range(PIECES):
                        x_copy(kind, half, direction, piece).start()

    def share_own(plane):
        reader, kind, half = goes(plane)

        @pl.when((reader == y) & (kind == core))
        def _():
            share_home(kind, half).start()

    moves = ((0, 0, x < NX - 1), (0, 1, x == 2), (1, 1, x > 0), (1, 0, x == 1))
    kind_from = (jnp.where(x > 0, 0, 1), jnp.where(x < NX - 1, 1, 0))

    def pass_on(plane):
        reader, kind, half = goes(plane)
        for source in range(2):
            @pl.when((reader == y) & (kind == kind_from[source]))
            def _():
                for place_of in range(PIECES):
                    x_copy(kind, half, source, place_of).wait_recv()
                    for direction, piece, when in moves:
                        if direction == source and piece == place_of:
                            @pl.when(when)
                            def _():
                                forward(direction, half, piece).start()
                share_near(source, half).start()

    for hops in (2, 1):
        for chunk in range(CHUNKS):
            z_copy(own, hops, hops, True, chunk).start()
            z_copy(own, hops, hops, False, chunk).start()
    hand_on(own, z, 0)
    for copy in small_copies:
        copy.start()
    tile_copy.start()
    weight_copy.start()

    def distance(q):
        return q + 2 * (q % 2) - 1

    def at_lag(t, lag, act):
        q = t - lag
        d = distance(jnp.maximum(q, 1))

        @pl.when(q == 0)
        def _():
            act(z)

        @pl.when((q > 0) & (q <= FAR))
        def _():
            act((z + NZ - d) % NZ)

            @pl.when(d < FAR)
            def _():
                act((z + d) % NZ)

    def z_step(t):
        d = distance(t)
        even = d % 2 == 0
        for chunk in range(CHUNKS):
            z_copy(own, d, 1, True, chunk).wait_recv()

            @pl.when(even & (d < FAR))
            def _():
                z_copy(up.at[d], d + 2, 2, True, chunk).start()

            @pl.when(d < FAR)
            def _():
                z_copy(own, d, 1, False, chunk).wait_recv()

                @pl.when(even & (d < FAR - 2))
                def _():
                    z_copy(down.at[d], d + 2, 2, False, chunk).start()

        @pl.when(even & (d < FAR))
        def _():
            for chunk in range(CHUNKS):
                z_copy(up.at[d], d + 1, 1, True, chunk).start()
                z_copy(down.at[d], d + 1, 1, False, chunk).start()

        hand_on(up.at[d], (z + NZ - d) % NZ, d)

        @pl.when(d < FAR)
        def _():
            hand_on(down.at[d], (z + d) % NZ, FAR + d)

    def loop_body(t, carry):
        @pl.when(t <= FAR)
        def _():
            z_step(t)

        at_lag(t, Y_LAG, complete)

        @pl.when(t == SYNC)
        def _():
            @pl.when(core == 0)
            def _():
                pl.semaphore_wait(barrier, 1)

            share_own(z)

            def earlier(d, nothing):
                share_own((z + d) % NZ)
                share_own((z + NZ - d) % NZ)
                return nothing

            lax.fori_loop(1, SYNC - Y_LAG + 1, earlier, 0)

        @pl.when(t > SYNC)
        def _():
            at_lag(t, Y_LAG, share_own)

        at_lag(t, F_LAG, pass_on)
        return carry

    lax.fori_loop(1, 3, loop_body, 0)

    rows = own.shape[0]
    entries = STEPS * slots
    lanes = draft.shape[1]
    lane = lax.broadcasted_iota(jnp.int32, (1, lanes), 1)
    deep = lax.broadcasted_iota(jnp.int32, (lanes, lanes), 0)
    wide = lax.broadcasted_iota(jnp.int32, (lanes, lanes), 1)

    def upright(line):
        spread = jnp.where(deep == wide, jnp.broadcast_to(line, (lanes, lanes)), 0)
        return jnp.sum(spread, axis=1, keepdims=True)

    def falling(grid):
        return jnp.sum(grid, axis=0, keepdims=True)

    for copy in small_copies:
        copy.wait()
    pad = jnp.zeros((2, lanes - entries), jnp.int32)
    places = jnp.concatenate([coords[...], pad], axis=1)
    of_step = lane // slots
    slot = lane - of_step * slots
    limit = jnp.zeros_like(lane)
    for s in range(STEPS):
        limit = jnp.where(of_step == s, counts[0, s], limit)
    row_block = jnp.where(slot < limit, places[0:1, :], BLOCKS)
    column_block = places[1:2, :]
    key = of_step * (2 * BLOCKS) + row_block
    full = key * lanes + lane
    key_up = upright(key)
    rank_up = jnp.sum(
        (jnp.broadcast_to(full, (lanes, lanes)) < upright(full)).astype(jnp.int32),
        axis=1, keepdims=True,
    )
    hit = rank_up == wide
    order = falling(jnp.where(hit, deep, 0))
    spot_up = upright((column_block % NZH) * NY + column_block // NZH)
    ranked = falling(jnp.where(hit, key_up, 0))
    follows = (ranked == pltpu.roll(ranked, 1, 1)) & (lane > 0)
    goal = (lane // BLOCKS) * (2 * BLOCKS) + lane % BLOCKS
    upto = falling(((key_up <= goal) & (deep < entries)).astype(jnp.int32))
    some = falling(((key_up == goal) & (deep < entries)).astype(jnp.int32))
    draft[0:1, :] = order
    draft[1:2, :] = falling(jnp.where(hit, spot_up, 0))
    draft[2:3, :] = follows.astype(jnp.int32)
    draft[3:4, :] = jnp.where(some > 0, upto, 0)
    table_copy = pltpu.make_async_copy(draft, table, d_sem)

    def multiply(ref, index, step):
        for k in range(slots):
            e = step * slots + k
            product = jnp.dot(
                tiles[table[0, e]], ref[index, table[1, e]],
                preferred_element_type=jnp.float32,
            )
            if k > 0:
                product += jnp.where(table[2, e] == 1, sums[e], 0.0)
            sums[e + 1] = product

    def step_of(shared, rel):
        other = (rel * 2 + STEPS - 1 + core * 2) % STEPS
        return shared * other + (1 - shared) * rel * 2

    lax.fori_loop(3, FAR + Y_LAG + 3, loop_body, 0)
    sums[0] = jnp.zeros(sums.shape[1:], sums.dtype)
    table_copy.start()
    table_copy.wait()
    tile_copy.wait()
    weight_copy.wait()
    for half in range(2):
        share(0, home.at[0], home.at[2], half).wait_recv()

    def home_body(i, carry):
        multiply(home, i * 2, step_of(i, 0))
        return carry

    lax.fori_loop(0, 2, home_body, 0)
    lax.fori_loop(FAR + Y_LAG + 3, FAR + F_LAG + 1, loop_body, 0)
    for half in range(2):
        for direction in range(2):
            share_near(direction, half).wait_recv()

    def near_body(i, carry):
        multiply(near, i, step_of(i // 2, 1 + 2 * (i % 2)))
        return carry

    lax.fori_loop(0, 4, near_body, 0)
    early = [step_of(shared, rel) for shared in range(2) for rel in (0, 1, 3)]
    late = [step_of(shared, 2) for shared in range(2)]

    def base_body(block, carry):
        held = sums[table[3, block + early[0] * BLOCKS]]
        for step in early[1:]:
            held += sums[table[3, block + step * BLOCKS]]
        base[block] = held
        return carry

    lax.fori_loop(0, BLOCKS, base_body, 0)
    for half in range(2):
        for piece in range(2):
            forward(0, half, piece).wait_recv()
            share_across(half, piece).start()
    multiply(across, 0, step_of(0, 2))
    for half in range(2):
        for piece in range(PIECES):
            share_across(half, piece).wait_recv()
    multiply(beyond, 0, step_of(1, 2))

    span = rows // PARTS

    def total(block, at):
        held = base[block, at]
        for step in late:
            held += sums[table[3, block + step * BLOCKS], at]
        return held

    def g_copy(turn, i, p):
        at = pl.ds(p * span, span)
        return remote(
            give.at[turn, i, at], got.at[turn, i, at], g_send.at[turn, i, p],
            g_recv.at[turn, i, p], device(x, core, others[i], z),
        )

    def across_z(p):
        at = pl.ds(p * span, span)
        return remote(z_give.at[at], z_got.at[at], z_send.at[p], z_recv.at[p], partner)

    halves = (1 - zh, zh)
    cuts = [pl.ds(p * span, span) for p in range(PARTS)]
    for turn in range(2):
        for p in range(PARTS):
            for i in (1, 0, 2):
                give[turn, i, cuts[p]] = total(
                    others[i] * NZH + halves[turn], cuts[p]
                ).astype(give.dtype)
                g_copy(turn, i, p).start()

    def gathered(turn, p):
        held = total(y * NZH + halves[turn], cuts[p])
        for i in range(NY - 1):
            g_copy(turn, i, p).wait_recv()
        for i in range(NY - 1):
            held += got[turn, i, cuts[p]].astype(jnp.float32)
        return held

    for p in range(PARTS):
        z_give[cuts[p]] = gathered(0, p).astype(z_give.dtype)
        across_z(p).start()
    for p in range(PARTS):
        hold[cuts[p]] = gathered(1, p)
    for p in range(PARTS):
        across_z(p).wait()
        aggregated = (hold[cuts[p]] + z_got[cuts[p]].astype(jnp.float32)).astype(weight.dtype)
        product = jnp.dot(aggregated, weight[...], preferred_element_type=jnp.float32)
        out[cuts[p]] = jnp.maximum(product, 0.0).astype(out.dtype)

    for turn in range(2):
        for i in range(NY - 1):
            for p in range(PARTS):
                g_copy(turn, i, p).wait_send()
    for half in range(2):
        share(0, home.at[0], home.at[2], half).wait_send()
        for piece in range(PIECES):
            share_across(half, piece).wait_send()
        for direction in range(2):
            share_near(direction, half).wait_send()
            for kind in range(2):
                @pl.when(sends(kind, direction))
                def _():
                    for piece in range(PIECES):
                        x_copy(kind, half, direction, piece).wait_send()
        for direction, piece, when in moves:
            @pl.when(when)
            def _():
                forward(direction, half, piece).wait_send()

    def hand_on_done(src, plane, index):
        @pl.when(goes(plane)[0] != y)
        def _():
            y_copy(src, plane, index).wait_send()

    hand_on_done(own, z, 0)

    def drain(t, carry):
        hand_on_done(up.at[t], (z + NZ - t) % NZ, t)
        for chunk in range(CHUNKS):
            z_copy(own, t, 1, True, chunk).wait_send()

        @pl.when(t < FAR)
        def _():
            hand_on_done(down.at[t], (z + t) % NZ, FAR + t)
            for chunk in range(CHUNKS):
                z_copy(own, t, 1, False, chunk).wait_send()

        return carry

    lax.fori_loop(1, FAR + 1, drain, 0)


def local(features, weight, tile_values, tile_coords, tile_counts):
    rows, width = features.shape
    slots = tile_values.shape[0] // STEPS
    dma = pltpu.SemaphoreType.DMA
    kind = features.dtype
    vmem = pl.BlockSpec(memory_space=pltpu.VMEM)
    hbm = pl.BlockSpec(memory_space=pltpu.HBM)
    return pl.pallas_call(
        functools.partial(layer_kernel, slots=slots),
        out_shape=jax.ShapeDtypeStruct((rows, weight.shape[1]), kind),
        in_specs=[
            hbm, hbm, hbm, hbm, hbm,
        ],
        out_specs=vmem,
        scratch_shapes=[
            pltpu.VMEM((3, BLOCKS, rows, width), kind),
            pltpu.VMEM((4, BLOCKS, rows, width), kind),
            pltpu.VMEM((1, BLOCKS, rows, width), kind),
            pltpu.VMEM((1, BLOCKS, rows, width), kind),
            pltpu.VMEM((FAR + 1, rows, width), kind),
            pltpu.VMEM((FAR, rows, width), kind),
            pltpu.VMEM(tile_values.shape, kind),
            pltpu.VMEM((STEPS * slots + 1, rows, width), jnp.float32),
            pltpu.VMEM((2, NY - 1, rows, width), kind),
            pltpu.VMEM((2, NY - 1, rows, width), kind),
            pltpu.VMEM((rows, width), jnp.float32),
            pltpu.VMEM((rows, width), kind),
            pltpu.VMEM((rows, width), kind),
            pltpu.VMEM(weight.shape, kind),
            pltpu.VMEM((8, LANES), jnp.int32),
            pltpu.SMEM((8, LANES), jnp.int32),
            pltpu.SMEM(tile_counts.shape, jnp.int32),
            pltpu.VMEM(tile_coords.T.shape, jnp.int32),
            pltpu.VMEM((BLOCKS, rows, width), jnp.float32),
            dma((FAR + 1, CHUNKS)), dma((FAR + 1, CHUNKS)), dma((FAR, CHUNKS)), dma((FAR, CHUNKS)),
            dma((NZ,)), dma((4, NY)), dma((4,)),
            dma((2, 4, PIECES)), dma((2, 2, PIECES)), dma((2, 2, PIECES)), dma((2, PIECES)),
            dma((3 + PIECES, 2)), dma((3 + PIECES, 2)),
            dma((2, NY - 1, PARTS)), dma((2, NY - 1, PARTS)), dma((PARTS,)), dma((PARTS,)),
            dma, dma, dma, dma((2,)),
        ],
        compiler_params=pltpu.CompilerParams(
            collective_id=0, has_side_effects=True, vmem_limit_bytes=60 * 1024 * 1024
        ),
        name="layer",
    )(tile_counts, tile_coords.T, features, weight, tile_values)


def solution(mesh):
    placed = (
        P(("loop", "rep"), None),
        P(),
        P(("loop", "rep"), None, None),
        P(("loop", "rep"), None),
        P(("loop", "rep"), None),
    )
    return jax.shard_map(
        local, mesh=mesh, in_specs=placed, out_specs=P(("loop", "rep"), None), check_vma=False
    )
```
